128 devices in a mesh: obs: 4 (over x_hi, core), state: 32 (over y, x_lo, z).
Axes of the slice: x: 4 (x_hi: 2, x_lo: 2; x = x_hi * 2 + x_lo), y: 4, z: 4, core: 2. Of those that a mesh axis runs over, the one named last changes fastest.
Arguments:
- jacobian: bfloat16 [8192, 40960], P('obs', 'state'), may hold values from -0.125 to 0.125
- obs_weight: float32 [8192], P('obs'), may hold values from 0.25 to 4
- observed: float32 [8192], P('obs'), may hold values from -6 to 6
- prior_state: bfloat16 [40960], P('state'), may hold values from -1.1953125 to 1.1953125
- prior_std: bfloat16 [40960], P('state'), may hold values from 0.5 to 2
- owner_slot: int32 [40960], P('state'), may hold values from 0 to 40959, each once
Outputs:
- gram_band: float32 [32, 1280, 3, 1280], P('state', 'obs')
- gradient: float32 [40960], P('state')
The draws below stay inside these ranges and needn't reach their ends.
Inputs may be any that keep to these rules, and one draw needn't show every extreme that they name: owner_slot names every position once.
All inputs are finite; a program needn't handle non-finite values.
Results may differ from the reference program's by a relative error of at most 0.0028.
Values may be sent and summed in bfloat16 or wider, within the bound.
No kernel may reach another device: no remote copies, remote signals or barrier semaphores. Data moves between devices by JAX's collectives and lax.ppermute only.
A program may use at most 128 MiB of HBM per device.

```python
import math
import jax
import jax.numpy as jnp
from jax import lax

C = 1280
ROWS_DEV = 2048
ROWS = 8192
S = 40960
N_STATE = 32


def levels(rng, extent, split, smallest, largest):
    def one(dim, blocks):
        steps = jax.random.uniform(jax.random.fold_in(jax.random.fold_in(rng, 6), dim), (blocks,), jnp.float32, smallest / len(split), largest / len(split))
        return jnp.repeat(jnp.exp(steps), extent[dim] // blocks).reshape((-1,) + (1,) * (len(extent) - dim - 1))

    level = one(*split[0])
    for cut in split[1:]:
        level = level * one(*cut)
    return level


def bell_draw(key, dims, scale, limit, shards=(), held_as=jnp.bfloat16):
    drawn = scale * jax.random.normal(key, dims, jnp.float32)
    if shards:
        drawn = drawn * levels(key, dims, shards, -0.22, 0.18)
    return jnp.clip(drawn, -limit, limit).astype(held_as)


def setup_inputs(seed: int = 0) -> dict:
    arg_keys = jax.random.split(jax.random.key(seed), 7)
    jacobian = bell_draw(arg_keys[0], (ROWS, S), ROWS_DEV ** -0.5, 0.125, ((0, 4), (1, 32)))
    obs_weight = jnp.clip(jnp.exp(math.log(4.0) - 2.7725887 * jax.random.uniform(arg_keys[1], (ROWS,), jnp.float32) ** levels(arg_keys[1], (ROWS,), ((0, 4),), -0.2, 0.2)), 0.25, 4.0)
    observed = bell_draw(arg_keys[2], (ROWS,), 1.0, 6.0, ((0, 4),), jnp.float32)
    prior_state = bell_draw(arg_keys[3], (S,), 0.2, 1.1953125, ((0, 32),))
    prior_std = jnp.clip(jnp.exp(math.log(2.0) - 1.3862944 * jax.random.uniform(arg_keys[4], (S,), jnp.float32) ** levels(arg_keys[4], (S,), ((0, 32),), -0.2, 0.2)), 0.5, 2.0).astype(jnp.bfloat16)
    owner_slot = jax.random.permutation(arg_keys[5], S).astype(jnp.int32)
    return dict(jacobian=jacobian, obs_weight=obs_weight, observed=observed, prior_state=prior_state, prior_std=prior_std, owner_slot=owner_slot)


def reference(jacobian, obs_weight, observed, prior_state, prior_std, owner_slot):
    weighted = (jacobian * obs_weight[:, None]).astype(jnp.bfloat16)
    spread = prior_std.astype(jnp.float32)

    def one_block(block):
        left = lax.dynamic_slice_in_dim(weighted, (block * C).astype(jnp.int32), C, 1)
        rows_std = lax.dynamic_slice_in_dim(spread, (block * C).astype(jnp.int32), C, 0)
        parts = []
        for step in range(3):
            other = ((block + step) % N_STATE).astype(jnp.int32)
            right = lax.dynamic_slice_in_dim(jacobian, (other * C).astype(jnp.int32), C, 1)
            cols_std = lax.dynamic_slice_in_dim(spread, (other * C).astype(jnp.int32), C, 0)
            total = jnp.dot(left.T, right, preferred_element_type=jnp.float32)
            parts.append(total * rows_std[:, None] * cols_std[None, :])
        return jnp.stack(parts, axis=1)

    gram_band = lax.map(one_block, jnp.arange(N_STATE, dtype=jnp.int32))
    model = jnp.dot(jacobian, prior_state, preferred_element_type=jnp.float32)
    misfit = (obs_weight * (observed - model)).astype(jnp.bfloat16)
    descent = jnp.dot(misfit, jacobian, preferred_element_type=jnp.float32)
    gradient = jnp.zeros((S,), jnp.float32).at[owner_slot].set(spread * descent)
    return gram_band, gradient
```

```python
import jax
import jax.numpy as jnp
from jax import lax
from jax.experimental import pallas as pl
from jax.experimental.pallas import tpu as pltpu
from jax.sharding import PartitionSpec as P


N_OBS, N_STATE = 4, 32
C, R = 1280, 2048
Q = C // N_OBS
HALF = C // 2
BF, F32 = jnp.bfloat16, jnp.float32


def over_state(value, target):
    return lax.ppermute(value, "state", [(s, target(s)) for s in range(N_STATE)])


def over_obs(value, flip):
    return lax.ppermute(value, "obs", [(o, o ^ flip) for o in range(N_OBS)])


def over_both(value, flip, step):
    pairs = [
        (o * N_STATE + s, (o ^ flip) * N_STATE + (s + step) % N_STATE)
        for o in range(N_OBS)
        for s in range(N_STATE)
    ]
    return lax.ppermute(value, ("obs", "state"), pairs)


def near(k):
    return lambda s: s // 8 * 8 + (s + k) % 8


def far(k):
    return lambda s: (s + 8 * k) % N_STATE


def prepare_kernel(quarters, jac, weight, ws, wk, wp, wo, n1, n2, turned):
    block = jac[...]
    n1[...] = block[:, :HALF]
    n2[...] = block[:, HALF:]
    turned[...] = (block.astype(F32).T * weight[...]).astype(BF)

    def quarter(k):
        return turned[pl.ds(pl.multiple_of(quarters[k] * Q, Q), Q), :]

    ps, os, pk, ok = (quarter(k) for k in range(4))
    ws[:Q], ws[Q:] = ps, os
    wk[:Q], wk[Q:] = pk, ok
    wp[:Q], wp[Q:] = ps, pk
    wo[:Q], wo[Q:] = os, ok


def prepare(jacobian, obs_weight, quarters):
    rows = 256
    tall = jax.ShapeDtypeStruct((HALF, R), BF)
    cols = jax.ShapeDtypeStruct((R, HALF), BF)
    tall_spec = pl.BlockSpec((HALF, rows), lambda i, q: (0, i))
    cols_spec = pl.BlockSpec((rows, HALF), lambda i, q: (i, 0))
    return pl.pallas_call(
        prepare_kernel,
        out_shape=(tall,) * 4 + (cols,) * 2,
        grid_spec=pltpu.PrefetchScalarGridSpec(
            num_scalar_prefetch=1,
            grid=(R // rows,),
            in_specs=[
                pl.BlockSpec((rows, C), lambda i, q: (i, 0)),
                pl.BlockSpec((1, rows), lambda i, q: (0, i)),
            ],
            out_specs=(tall_spec,) * 4 + (cols_spec,) * 2,
            scratch_shapes=[pltpu.VMEM((C, rows), BF)],
        ),
        name="prepare",
    )(quarters, jacobian, obs_weight.reshape(1, R))


WIDE = 1024
LINES = C * N_STATE // WIDE


def place_kernel(base, slots, values, out):
    hi_ids = lax.broadcasted_iota(jnp.int32, (16, WIDE), 0)
    lo_ids = lax.broadcasted_iota(jnp.int32, (128, WIDE), 0)

    def body(line, total):
        local = slots[pl.ds(line, 1), :].astype(jnp.int32) - base[0]
        value = values[pl.ds(line, 1), :]
        first = value.astype(BF).astype(F32)
        second = (value - first).astype(BF).astype(F32)
        third = value - first - second
        mine = (local >> 7) == hi_ids
        rows = jnp.concatenate(
            [jnp.where(mine, part, 0.0) for part in (first, second, third)], axis=0
        ).astype(BF)
        spot = jnp.where((local & 127) == lo_ids, 1.0, 0.0).astype(BF)
        return total + lax.dot_general(
            rows, spot, (((1,), (1,)), ((), ())), preferred_element_type=F32
        )

    total = lax.fori_loop(0, LINES, body, jnp.zeros((48, 128), F32))
    out[...] = total[:16] + total[16:32] + total[32:]


def place(base, slots, values):
    full = pl.BlockSpec((LINES, WIDE), lambda i, b: (0, 0))
    out = pl.pallas_call(
        place_kernel,
        out_shape=jax.ShapeDtypeStruct((16, 128), F32),
        grid_spec=pltpu.PrefetchScalarGridSpec(
            num_scalar_prefetch=1,
            grid=(1,),
            in_specs=[full, full],
            out_specs=pl.BlockSpec((16, 128), lambda i, b: (0, 0)),
        ),
        name="place",
    )(base.reshape(1), slots.reshape(LINES, WIDE), values.reshape(LINES, WIDE))
    return out[: C // 128].reshape(C)


def dot(left, right):
    return jnp.dot(left, right, preferred_element_type=F32)


def on_device(jacobian, obs_weight, observed, prior_state, prior_std, owner_slot):
    group = lax.axis_index("obs").astype(jnp.int32)
    block = lax.axis_index("state").astype(jnp.int32)
    half, core = group // 2, group % 2
    ps = 2 * (1 - half) + 1 - core
    pk = 2 * (1 - half) + core
    os = 2 * half + 1 - core
    quarters = jnp.stack([ps, os, pk, group])
    spread = prior_std.astype(F32)
    rows_std = lax.dynamic_slice_in_dim(spread, group * Q, Q, 0)

    partial = dot(jacobian, prior_state)
    packet = jnp.concatenate([partial, owner_slot.astype(F32)])
    packets = [packet] + [over_state(packet, near(k)) for k in range(1, 8)]
    next_std = over_state(prior_std, lambda s: (s - 1) % N_STATE)
    after_std = over_state(prior_std, lambda s: (s - 2) % N_STATE)
    ws, wk, wp, wo, n1, n2 = prepare(jacobian, obs_weight, quarters)
    near_model = sum(p[:R] for p in packets)
    near_slots = jnp.concatenate([p[R:] for p in packets])
    packet = jnp.concatenate([near_model, near_slots])

    packet, n1, wp, n2, wo = lax.optimization_barrier((packet, n1, wp, n2, wo))
    n1 = over_state(n1, lambda s: (s - 1) % N_STATE)
    wp = over_state(wp, lambda s: (s + 1) % N_STATE)
    packets = [packet] + [over_state(packet, far(k)) for k in range(1, 4)]
    model = sum(p[:R] for p in packets)
    slots = jnp.concatenate([p[R:] for p in packets])
    misfit = (obs_weight * (observed - model)).astype(BF)
    descent = dot(misfit, jacobian)
    descent = sum([descent] + [over_obs(descent, k) for k in range(1, 4)])
    scaled = spread * descent
    n2 = over_state(n2, lambda s: (s - 1) % N_STATE)
    wo = over_state(wo, lambda s: (s + 1) % N_STATE)
    column = jnp.stack([scaled] + [over_state(scaled, far(k)) for k in range(1, 4)])
    values = jnp.stack([column] + [over_state(column, near(k)) for k in range(1, 8)], axis=1)
    gradient = place(block * C, slots, values.reshape(-1))

    def reduced(right):
        got = over_obs(dot(ws, right), 1)
        total = dot(wk, right) + got
        other = over_obs(total[:Q].astype(BF), 2)
        return total[Q:] + other.astype(F32)

    def passed_on(left, right, flip):
        got = over_obs(dot(left[:Q], right), 1)
        total = dot(left[Q:], right) + got
        return over_both(total.astype(BF), flip, -1).astype(F32)

    slab0 = reduced(jacobian)
    slab1 = jnp.concatenate([reduced(n1), reduced(n2)], axis=1)
    slab2 = jnp.concatenate(
        [passed_on(wp, n, 2) + passed_on(wo, n, 0) for n in (n1, n2)], axis=1
    )
    stds = (spread, next_std.astype(F32), after_std.astype(F32))
    band = jnp.stack(
        [
            slab * rows_std[:, None] * std[None, :]
            for slab, std in zip((slab0, slab1, slab2), stds)
        ],
        axis=1,
    )
    return (band[None], gradient)


def solution(mesh):
    placed = (P("obs", "state"), P("obs"), P("obs"), P("state"), P("state"), P("state"))
    return jax.shard_map(
        on_device,
        mesh=mesh,
        in_specs=placed,
        out_specs=(P("state", "obs", None, None), P("state")),
        check_vma=False,
    )
```

```python
import functools

import jax
import jax.numpy as jnp
from jax import lax
from jax.experimental import pallas as pl
from jax.experimental.pallas import tpu as pltpu
from jax.sharding import PartitionSpec as P


N_OBS, N_STATE = 4, 32
C, R = 1280, 2048
Q = C // N_OBS
HALF = C // 2
WIDE = 768
BF, F32 = jnp.bfloat16, jnp.float32


def over_state(value, target):
    return lax.ppermute(value, "state", [(s, target(s)) for s in range(N_STATE)])


def over_obs(value, flip):
    return lax.ppermute(value, "obs", [(o, o ^ flip) for o in range(N_OBS)])


def over_both(value, flip, target):
    pairs = [
        (o * N_STATE + s, (o ^ flip) * N_STATE + target(s))
        for o in range(N_OBS)
        for s in range(N_STATE)
    ]
    return lax.ppermute(value, ("obs", "state"), pairs)


def back(s):
    return (s - 1) % N_STATE


def along_z(k):
    return lambda s: s // 4 * 4 + (s + k) % 4


def along_x(s):
    return s ^ 4


def ring_y(s):
    return (s + 8 if s & 4 else s - 8) % N_STATE


def along_y(k):
    return lambda s: (s + 8 * k) % N_STATE


ROWS = 512


def prepare_kernel(picks, jac, weight, tall, cols, select, *, start):
    @pl.when(pl.program_id(0) == 0)
    def _():
        place = lax.broadcasted_iota(jnp.int32, (HALF, HALF), 0)
        source = lax.broadcasted_iota(jnp.int32, (HALF, HALF), 1)
        moved = jnp.where(picks[1] == 0, Q, 0)
        wanted = jnp.where(place < Q, place + moved, place - moved)
        select[...] = jnp.where(wanted == source, 1.0, 0.0).astype(BF)

    block = jac[...]
    cols[...] = block[:, start : start + cols.shape[1]]
    chosen = jnp.where(picks[0] == 0, block[:, :HALF], block[:, HALF:])
    turned = lax.dot_general(
        select[...], chosen, (((1,), (1,)), ((), ())), preferred_element_type=F32
    )
    tall[...] = (turned * weight[...]).astype(BF)


def prepare(jacobian, obs_weight, half, core, start, width):
    return pl.pallas_call(
        functools.partial(prepare_kernel, start=start),
        out_shape=(jax.ShapeDtypeStruct((HALF, R), BF), jax.ShapeDtypeStruct((R, width), BF)),
        grid_spec=pltpu.PrefetchScalarGridSpec(
            num_scalar_prefetch=1,
            grid=(R // ROWS,),
            in_specs=[
                pl.BlockSpec((ROWS, C), lambda i, q: (i, 0)),
                pl.BlockSpec((1, ROWS), lambda i, q: (0, i)),
            ],
            out_specs=(
                pl.BlockSpec((HALF, ROWS), lambda i, q: (0, i)),
                pl.BlockSpec((ROWS, width), lambda i, q: (i, 0)),
            ),
            scratch_shapes=[pltpu.VMEM((HALF, HALF), BF)],
        ),
    )(jnp.stack([half, core]), jacobian, obs_weight.reshape(1, R))


LINES = C // 128
PACKET = 24


def place_kernel(base, packets, out):
    hi_ids = lax.broadcasted_iota(jnp.int32, (16, C), 0)
    lo_ids = lax.broadcasted_iota(jnp.int32, (128, C), 0).astype(F32).astype(BF)
    one, zero = jnp.ones((128, C), BF), jnp.zeros((128, C), BF)

    def row(packet, first):
        return jnp.concatenate(
            [packet[first + k : first + k + 1, :] for k in range(LINES)], axis=1
        )

    def body(source, total):
        packet = packets[source]
        local = row(packet, 0).astype(jnp.int32) - base[0]
        value = row(packet, LINES)
        first = value.astype(BF).astype(F32)
        second = (value - first).astype(BF).astype(F32)
        third = value - first - second
        mine = (local >> 7) == hi_ids
        rows = jnp.concatenate(
            [jnp.where(mine, part, 0.0) for part in (first, second, third)], axis=0
        ).astype(BF)
        lane = (local & 127).astype(F32).astype(BF)
        spot = jnp.where(lane == lo_ids, one, zero)
        return total + lax.dot_general(
            rows, spot, (((1,), (1,)), ((), ())), preferred_element_type=F32
        )

    total = lax.fori_loop(0, N_STATE, body, jnp.zeros((48, 128), F32), unroll=4)
    total = total[:16] + total[16:32] + total[32:]
    for line in range(LINES):
        out[line * 128 : (line + 1) * 128] = total[line]


def place(base, packets):
    return pl.pallas_call(
        place_kernel,
        out_shape=jax.ShapeDtypeStruct((C,), F32),
        grid_spec=pltpu.PrefetchScalarGridSpec(
            num_scalar_prefetch=1,
            grid=(1,),
            in_specs=[pl.BlockSpec((N_STATE, PACKET, 128), lambda i, b: (0, 0, 0))],
            out_specs=pl.BlockSpec((C,), lambda i, b: (0,)),
        ),
        name="place",
    )(base.reshape(1), packets)


def same_kernel(source, out):
    out[...] = source[...]


def same(value):
    return pl.pallas_call(
        same_kernel, out_shape=jax.ShapeDtypeStruct(value.shape, value.dtype), name="same"
    )(value)


def dot(left, right):
    return jnp.dot(left, right, preferred_element_type=F32)


def whole(value):
    return pl.BlockSpec(value.shape, lambda i: (0,) * value.ndim)


def rows_of(shape):
    return pl.BlockSpec((Q, shape[1]), lambda i: (i, 0))


def pick(value, k):
    return pl.BlockSpec((Q, value.shape[1]), lambda i: (k, 0))


def product_kernel(first, second, right, out):
    @pl.when(pl.program_id(0) == 0)
    def _():
        out[...] = dot(first[...], right[...])

    @pl.when(pl.program_id(0) == 1)
    def _():
        out[...] = dot(second[...], right[...])


def product(first, second, right):
    shape = (HALF, right.shape[1])
    return pl.pallas_call(
        product_kernel,
        grid=(2,),
        out_shape=jax.ShapeDtypeStruct(shape, F32),
        in_specs=[pick(first, 0), pick(second, 0), whole(right)],
        out_specs=rows_of(shape),
    )(first, second, right)


def closing_kernel(first, second, right, got, part, own):
    @pl.when(pl.program_id(0) == 0)
    def _():
        part[...] = (dot(first[...], right[...]) + got[...]).astype(BF)

    @pl.when(pl.program_id(0) == 1)
    def _():
        own[...] = dot(second[...], right[...]) + got[...]


def closing(first, second, right, got):
    shapes = [jax.ShapeDtypeStruct((Q, right.shape[1]), dtype) for dtype in (BF, F32)]
    return pl.pallas_call(
        closing_kernel,
        grid=(2,),
        out_shape=tuple(shapes),
        in_specs=[pick(first, 1), pick(second, 1), whole(right), rows_of(got.shape)],
        out_specs=tuple(whole(shape) for shape in shapes),
    )(first, second, right, got)


def split_kernel(left, *refs):
    rights, (sent, kept) = refs[:-2], refs[-2:]
    start = 0
    for right in rights:
        cols = slice(start, start + right.shape[1])
        start = cols.stop
        value = dot(left[...], right[...])

        @pl.when(pl.program_id(0) == 0)
        def _():
            sent[:, cols] = value

        @pl.when(pl.program_id(0) == 1)
        def _():
            kept[:, cols] = value


def split_product(left, rights):
    shape = jax.ShapeDtypeStruct((Q, sum(right.shape[1] for right in rights)), F32)
    return pl.pallas_call(
        split_kernel,
        grid=(2,),
        out_shape=(shape,) * 2,
        in_specs=[rows_of(left.shape)] + [whole(right) for right in rights],
        out_specs=(whole(shape),) * 2,
    )(left, *rights)


SLAB_STEPS = 4


def band_kernel(own0, x0, own1, x1, own2, x2, near, far, both, rows, here, ahead, band):
    scale = rows[...]
    band[0] = (own0[...] + x0[...].astype(F32)) * scale * here[...]
    left = own1[...] + x1[...].astype(F32)
    right = own2[...] + x2[...].astype(F32)
    band[1] = jnp.concatenate([left, right], axis=1) * scale * ahead[...]
    total = jnp.concatenate([near[...], far[...]], axis=1).astype(F32)
    band[2] = (total + both[...].astype(F32)) * scale


def finish(parts, rows, here, ahead):
    size = Q // SLAB_STEPS
    specs = [pl.BlockSpec((size, p.shape[1]), lambda i: (i, 0)) for p in parts]
    line = pl.BlockSpec((1, C), lambda i: (0, 0))
    return pl.pallas_call(
        band_kernel,
        grid=(SLAB_STEPS,),
        out_shape=jax.ShapeDtypeStruct((3, Q, C), F32),
        in_specs=specs + [pl.BlockSpec((size, 1), lambda i: (i, 0)), line, line],
        out_specs=pl.BlockSpec((3, size, C), lambda i: (0, i, 0)),
        name="finish",
    )(*parts, rows[:, None], here[None, :], ahead[None, :])


REST = C - WIDE


def copies(sources, targets, sems, first):
    made = []
    for k, (source, target) in enumerate(zip(sources, targets)):
        made.append(pltpu.make_async_copy(source, target, sems.at[first + k]))
        made[-1].start()
    return made


def sent_both_kernel(po, n1, n2, b1, v_po, v1, v2, o1, sems):
    loads = copies([po.at[pl.ds(0, Q)], n2, n1], [v_po, v2, v1], sems, 0)
    for load in loads[:2]:
        load.wait()
    o1[:, WIDE:] = dot(v_po[...], v2[...])
    loads[2].wait()
    o1[:, :WIDE] = dot(v_po[...], v1[...])
    copies([o1], [b1], sems, 3)[0].wait()


def sent_rest_kernel(wp, wo, pp, n2, k2, b01, v_wp, v_wo, v_pp, v2, ok2, o01, sems):
    top = pl.ds(0, Q)
    sources = [n2, wp.at[top], wo.at[top], pp.at[top]]
    loads = copies(sources, [v2, v_wp, v_wo, v_pp], sems, 0)
    for load in loads[:2]:
        load.wait()
    ok2[:Q] = dot(v_wp[...], v2[...])
    loads[2].wait()
    ok2[Q:] = dot(v_wo[...], v2[...])
    stores = copies([ok2], [k2], sems, 4)
    loads[3].wait()
    o01[...] = dot(v_pp[...], v2[...])
    stores += copies([o01], [b01], sems, 5)
    for store in stores:
        store.wait()


def kept_both_kernel(po, n1, n2, got, scale, b1, v_po, v1, v2, o1, sems):
    loads = copies([po.at[pl.ds(Q, Q)], n2, n1], [v_po, v2, v1], sems, 0)
    for load in loads[:2]:
        load.wait()
    right = dot(v_po[...], v2[...]) + got[:, WIDE:]
    o1[:, WIDE:] = (right * scale[:, WIDE:]).astype(BF)
    loads[2].wait()
    left = dot(v_po[...], v1[...]) + got[:, :WIDE]
    o1[:, :WIDE] = (left * scale[:, :WIDE]).astype(BF)
    copies([o1], [b1], sems, 3)[0].wait()


def kept_rest_kernel(wp, pp, n2, g2, g01, scale, part, b01, *scratch):
    v_wp, v_pp, v2, o_part, o01, sems = scratch
    low = pl.ds(Q, Q)
    loads = copies([n2, wp.at[low], pp.at[low]], [v2, v_wp, v_pp], sems, 0)
    for load in loads[:2]:
        load.wait()
    o_part[...] = (dot(v_wp[...], v2[...]) + g2[:Q]).astype(BF)
    stores = copies([o_part], [part], sems, 3)
    loads[2].wait()
    far = dot(v_pp[...], v2[...]) + g01[...]
    o01[...] = (far * scale[:, WIDE:]).astype(BF)
    stores += copies([o01], [b01], sems, 4)
    for store in stores:
        store.wait()


def own_kernel(left, right, got, own):
    own[...] = dot(left[...], right[...]) + got[...]


def own_product(left, right, got):
    shape = jax.ShapeDtypeStruct((Q, right.shape[1]), F32)
    return pl.pallas_call(
        own_kernel,
        grid=(1,),
        out_shape=shape,
        in_specs=[pick(left, 1), whole(right), pick(got, 1)],
        out_specs=whole(shape),
    )(left, right, got)


def vmem(*shapes):
    return [pltpu.VMEM(shape, dtype) for shape, dtype in shapes]


ANYWHERE = pl.BlockSpec(memory_space=pl.ANY)
LEFT, NEAR, FAR = ((Q, R), BF), ((R, WIDE), BF), ((R, REST), BF)


def by_hand(kernel, operands, near, outs, loaded):
    shapes = [jax.ShapeDtypeStruct(*item) for item in outs]
    return pl.pallas_call(
        kernel,
        out_shape=tuple(shapes),
        in_specs=[ANYWHERE] * len(operands) + [pl.BlockSpec(memory_space=pltpu.VMEM)] * len(near),
        out_specs=(ANYWHERE,) * len(outs),
        scratch_shapes=vmem(*loaded, *outs)
        + [pltpu.SemaphoreType.DMA((len(loaded) + len(outs),))],
    )(*operands, *near)


def on_device(jacobian, obs_weight, observed, prior_state, prior_std, owner_slot):
    group = lax.axis_index("obs").astype(jnp.int32)
    block = lax.axis_index("state").astype(jnp.int32)
    half, core = group // 2, group % 2
    spread = prior_std.astype(F32)
    rows_std = lax.dynamic_slice_in_dim(spread, group * Q, Q, 0)

    next_std = over_state(prior_std, back).astype(F32)
    model = dot(jacobian, prior_state)
    wp, n1 = prepare(jacobian, obs_weight, 1 - half, core, 0, WIDE)
    model = model + sum(over_state(model, along_z(k)) for k in range(1, 4))
    model = model + over_state(model, along_x)
    model = model + sum(over_state(model, along_y(k)) for k in range(1, 4))
    misfit = (obs_weight * (observed - model)).astype(BF)
    descent = dot(misfit, jacobian)

    def packed(slots, values):
        parts = (slots.reshape(LINES, 128), values.reshape(LINES, 128))
        return jnp.concatenate(parts + (jnp.zeros((PACKET - 2 * LINES, 128), F32),))[None]

    descent = descent + over_obs(descent, 1)
    scaled = spread * descent
    slots = owner_slot.astype(F32)
    mine = jnp.concatenate([slots, scaled])
    other = over_both(mine, 0, lambda s: s ^ 4)
    scaled = scaled + over_both(scaled, 2, lambda s: s)
    other_scaled = other[C:] + over_both(mine[C:], 2, lambda s: s ^ 4)
    packet = jnp.concatenate([packed(slots, scaled), packed(other[:C], other_scaled)])

    packet, wp, n1 = lax.optimization_barrier((packet, wp, n1))
    next1 = over_state(n1, back)
    prev_p = over_state(wp, lambda s: (s + 1) % N_STATE)
    wo, n2 = prepare(jacobian, obs_weight, half, core, WIDE, C - WIDE)
    next2 = over_state(n2, back)
    prev_o = over_state(wo, lambda s: (s + 1) % N_STATE)
    packets = [packet]
    for _ in range(3):
        packets.append(over_state(packets[-1], ring_y))
    packet = same(jnp.concatenate(packets))
    packet = jnp.concatenate(
        [packet] + [over_state(packet, along_z(k)) for k in range(1, 4)]
    )
    gradient = place(block * C, packet)

    def exchanged(right):
        sent = product(wp, wo, right)
        got = over_obs(sent, 1)
        part, own = closing(wp, wo, right, got)
        return own, over_obs(part, 2)

    def returned(left, rights, flip, scales):
        sent, kept = split_product(left, rights)
        got = over_obs(sent, 1)
        part = ((kept + got) * scales[None, :]).astype(BF)
        return over_both(part, flip, back)

    own0, x0 = exchanged(jacobian)
    own1, x1 = exchanged(next1)
    spread = same(spread)
    rows_std = same(rows_std)
    b00 = returned(prev_p, [next1], 2, next_std[:WIDE])
    next_std = same(next_std)
    both = (prev_o, next1, next2)
    rest = (wp, wo, prev_p, next2)
    scale = next_std[None, :]
    (sent1,) = by_hand(sent_both_kernel, both, (), [((Q, C), F32)], [LEFT, NEAR, FAR])
    got1 = over_obs(sent1, 1)
    outs = [((HALF, REST), F32), ((Q, REST), F32)]
    sent2 = by_hand(sent_rest_kernel, rest, (), outs, [LEFT, LEFT, LEFT, FAR])
    got2 = [over_obs(value, 1) for value in sent2]
    outs = [((Q, C), BF)]
    (b1,) = by_hand(kept_both_kernel, both, (got1, scale), outs, [LEFT, NEAR, FAR])
    b1 = over_both(b1, 0, back)
    outs = [((Q, REST), BF)] * 2
    operands = (wp, prev_p, next2)
    part, b01 = by_hand(kept_rest_kernel, operands, (*got2, scale), outs, [LEFT, LEFT, FAR])
    x2 = over_obs(part, 2)
    b01 = over_both(b01, 2, back)

    own2 = own_product(wo, next2, got2[0])

    parts = (own0, x0, own1, x1, own2, x2, b00, b01, b1)
    band = finish(parts, rows_std, spread, next_std)
    return (jnp.transpose(band, (1, 0, 2))[None], gradient)


def solution(mesh):
    placed = (P("obs", "state"), P("obs"), P("obs"), P("state"), P("state"), P("state"))

    return jax.shard_map(
        on_device,
        mesh=mesh,
        in_specs=placed,
        out_specs=(P("state", "obs", None, None), P("state")),
        check_vma=False,
    )
```

```python
import functools

import jax
import jax.numpy as jnp
from jax import lax
from jax.experimental import pallas as pl
from jax.experimental.pallas import tpu as pltpu
from jax.sharding import PartitionSpec as P


N_OBS, N_STATE = 4, 32
C, R = 1280, 2048
Q = C // N_OBS
HALF = C // 2
WIDE = 768
BF, F32 = jnp.bfloat16, jnp.float32


def over_state(value, target):
    return lax.ppermute(value, "state", [(s, target(s)) for s in range(N_STATE)])


def over_obs(value, flip):
    return lax.ppermute(value, "obs", [(o, o ^ flip) for o in range(N_OBS)])


def over_both(value, flip, target):
    pairs = [
        (o * N_STATE + s, (o ^ flip) * N_STATE + target(s))
        for o in range(N_OBS)
        for s in range(N_STATE)
    ]
    return lax.ppermute(value, ("obs", "state"), pairs)


def back(s):
    return (s - 1) % N_STATE


def along_z(k):
    return lambda s: s // 4 * 4 + (s + k) % 4


def along_x(s):
    return s ^ 4


def ring_y(s):
    return (s + 8 if s & 4 else s - 8) % N_STATE


def along_y(k):
    return lambda s: (s + 8 * k) % N_STATE


ROWS = 512


def columns_kernel(jac, cols, *, start):
    cols[...] = jac[:, start : start + cols.shape[1]]


def columns(jacobian, start, width):
    seen = C if start else width
    return pl.pallas_call(
        functools.partial(columns_kernel, start=start),
        out_shape=jax.ShapeDtypeStruct((R, width), BF),
        grid=(R // ROWS,),
        in_specs=[pl.BlockSpec((ROWS, seen), lambda i: (i, 0))],
        out_specs=pl.BlockSpec((ROWS, width), lambda i: (i, 0)),
    )(jacobian)


def turn_kernel(half, core, jac, weight, tall, select):
    @pl.when(pl.program_id(0) == 0)
    def _():
        place = lax.broadcasted_iota(jnp.int32, (HALF, HALF), 0)
        source = lax.broadcasted_iota(jnp.int32, (HALF, HALF), 1)
        moved = jnp.where(core[0] == 0, Q, 0)
        wanted = jnp.where(place < Q, place + moved, place - moved)
        select[...] = jnp.where(wanted == source, 1.0, 0.0).astype(BF)

    turned = lax.dot_general(
        select[...], jac[...], (((1,), (1,)), ((), ())), preferred_element_type=F32
    )
    tall[...] = (turned * weight[...]).astype(BF)


def turn(jacobian, obs_weight, half, core):
    return pl.pallas_call(
        turn_kernel,
        out_shape=jax.ShapeDtypeStruct((HALF, R), BF),
        grid_spec=pltpu.PrefetchScalarGridSpec(
            num_scalar_prefetch=2,
            grid=(R // ROWS,),
            in_specs=[
                pl.BlockSpec((ROWS, HALF), lambda i, h, c: (i, h[0])),
                pl.BlockSpec((1, ROWS), lambda i, h, c: (0, i)),
            ],
            out_specs=pl.BlockSpec((HALF, ROWS), lambda i, h, c: (0, i)),
            scratch_shapes=[pltpu.VMEM((HALF, HALF), BF)],
        ),
    )(half.reshape(1), core.reshape(1), jacobian, obs_weight.reshape(1, R))


LINES = C // 128
PACKET = 24


def place_kernel(base, packets, out):
    hi_ids = lax.broadcasted_iota(jnp.int32, (16, C), 0)
    lo_ids = lax.broadcasted_iota(jnp.int32, (128, C), 0).astype(F32).astype(BF)
    one, zero = jnp.ones((128, C), BF), jnp.zeros((128, C), BF)

    def row(packet, first):
        return jnp.concatenate(
            [packet[first + k : first + k + 1, :] for k in range(LINES)], axis=1
        )

    def body(source, total):
        packet = packets[source]
        local = row(packet, 0).astype(jnp.int32) - base[0]
        value = row(packet, LINES)
        first = value.astype(BF).astype(F32)
        second = (value - first).astype(BF).astype(F32)
        third = value - first - second
        mine = (local >> 7) == hi_ids
        rows = jnp.concatenate(
            [jnp.where(mine, part, 0.0) for part in (first, second, third)], axis=0
        ).astype(BF)
        lane = (local & 127).astype(F32).astype(BF)
        spot = jnp.where(lane == lo_ids, one, zero)
        return total + lax.dot_general(
            rows, spot, (((1,), (1,)), ((), ())), preferred_element_type=F32
        )

    total = lax.fori_loop(0, N_STATE, body, jnp.zeros((48, 128), F32), unroll=4)
    total = total[:16] + total[16:32] + total[32:]
    for line in range(LINES):
        out[line * 128 : (line + 1) * 128] = total[line]


def place(base, packets):
    return pl.pallas_call(
        place_kernel,
        out_shape=jax.ShapeDtypeStruct((C,), F32),
        grid_spec=pltpu.PrefetchScalarGridSpec(
            num_scalar_prefetch=1,
            grid=(1,),
            in_specs=[pl.BlockSpec((N_STATE, PACKET, 128), lambda i, b: (0, 0, 0))],
            out_specs=pl.BlockSpec((C,), lambda i, b: (0,)),
        ),
        name="place",
    )(base.reshape(1), packets)


def same_kernel(source, out):
    out[...] = source[...]


def same(value):
    return pl.pallas_call(
        same_kernel, out_shape=jax.ShapeDtypeStruct(value.shape, value.dtype), name="same"
    )(value)


def dot(left, right):
    return jnp.dot(left, right, preferred_element_type=F32)


def whole(value):
    return pl.BlockSpec(value.shape, lambda i: (0,) * value.ndim)


def rows_of(shape):
    return pl.BlockSpec((Q, shape[1]), lambda i: (i, 0))


def pick(value, k):
    return pl.BlockSpec((Q, value.shape[1]), lambda i: (k, 0))


def product_kernel(first, second, right, out):
    @pl.when(pl.program_id(0) == 0)
    def _():
        out[...] = dot(first[...], right[...])

    @pl.when(pl.program_id(0) == 1)
    def _():
        out[...] = dot(second[...], right[...])


def product_kernel_once(left, right, out):
    out[...] = dot(left[...], right[...])


def product(first, second, right):
    shape = (HALF, right.shape[1])
    return pl.pallas_call(
        product_kernel,
        grid=(2,),
        out_shape=jax.ShapeDtypeStruct(shape, F32),
        in_specs=[pick(first, 0), pick(second, 0), whole(right)],
        out_specs=rows_of(shape),
    )(first, second, right)


def closing_kernel(first, second, right, got, part, own):
    @pl.when(pl.program_id(0) == 0)
    def _():
        part[...] = (dot(first[...], right[...]) + got[...]).astype(BF)

    @pl.when(pl.program_id(0) == 1)
    def _():
        own[...] = dot(second[...], right[...]) + got[...]


def closing(first, second, right, got):
    shapes = [jax.ShapeDtypeStruct((Q, right.shape[1]), dtype) for dtype in (BF, F32)]
    return pl.pallas_call(
        closing_kernel,
        grid=(2,),
        out_shape=tuple(shapes),
        in_specs=[pick(first, 1), pick(second, 1), whole(right), rows_of(got.shape)],
        out_specs=tuple(whole(shape) for shape in shapes),
    )(first, second, right, got)


def split_kernel(left, *refs):
    rights, (sent, kept) = refs[:-2], refs[-2:]
    start = 0
    for right in rights:
        cols = slice(start, start + right.shape[1])
        start = cols.stop
        value = dot(left[...], right[...])

        @pl.when(pl.program_id(0) == 0)
        def _():
            sent[:, cols] = value

        @pl.when(pl.program_id(0) == 1)
        def _():
            kept[:, cols] = value


def split_product(left, rights):
    shape = jax.ShapeDtypeStruct((Q, sum(right.shape[1] for right in rights)), F32)
    return pl.pallas_call(
        split_kernel,
        grid=(2,),
        out_shape=(shape,) * 2,
        in_specs=[rows_of(left.shape)] + [whole(right) for right in rights],
        out_specs=(whole(shape),) * 2,
    )(left, *rights)


SLAB_STEPS = 4


def band_kernel(own0, x0, own1, x1, near1, near2, rows, here, ahead, band):
    scale = rows[...]
    rest = jnp.zeros((scale.shape[0], C - WIDE), F32)
    band[0] = (own0[...] + x0[...].astype(F32)) * scale * here[...]
    early = (own1[...] + x1[...].astype(F32)) * scale * ahead[:, :WIDE]
    band[1] = jnp.concatenate([early, rest], axis=1)
    left = near1[...].astype(F32) + near2[...].astype(F32)
    band[2] = jnp.concatenate([left * scale, rest], axis=1)


def finish(parts, rows, here, ahead):
    size = Q // SLAB_STEPS
    specs = [pl.BlockSpec((size, p.shape[1]), lambda i: (i, 0)) for p in parts]
    line = pl.BlockSpec((1, C), lambda i: (0, 0))
    return pl.pallas_call(
        band_kernel,
        grid=(SLAB_STEPS,),
        out_shape=jax.ShapeDtypeStruct((3, Q, C), F32),
        in_specs=specs + [pl.BlockSpec((size, 1), lambda i: (i, 0)), line, line],
        out_specs=pl.BlockSpec((3, size, C), lambda i: (0, i, 0)),
        name="finish",
    )(*parts, rows[:, None], here[None, :], ahead[None, :])


def late_kernel(own2, x2, far1, far2, rows, ahead, _, band):
    @pl.when(pl.program_id(1) == 0)
    def _():
        band[0] = (own2[...] + x2[...].astype(F32)) * rows[...] * ahead[...]

    @pl.when(pl.program_id(1) == 1)
    def _():
        band[0] = (far1[...].astype(F32) + far2[...].astype(F32)) * rows[...]


def finish_late(band, own2, x2, far1, far2, rows, ahead):
    width = 256
    first = WIDE // width
    block = pl.BlockSpec((Q, width), lambda j, i: (0, j))
    return pl.pallas_call(
        late_kernel,
        grid=((C - WIDE) // width, 2),
        out_shape=jax.ShapeDtypeStruct((3, Q, C), F32),
        in_specs=[
            block,
            block,
            block,
            block,
            pl.BlockSpec((Q, 1), lambda j, i: (0, 0)),
            pl.BlockSpec((1, width), lambda j, i: (0, j + first)),
            pl.BlockSpec(memory_space=pl.ANY),
        ],
        out_specs=pl.BlockSpec((1, Q, width), lambda j, i: (1 + i, 0, j + first)),
        input_output_aliases={6: 0},
        name="finish_late",
    )(own2, x2, far1, far2, rows[:, None], ahead[None, :], band)


REST = C - WIDE


def copies(sources, targets, sems, first):
    made = []
    for k, (source, target) in enumerate(zip(sources, targets)):
        made.append(pltpu.make_async_copy(source, target, sems.at[first + k]))
        made[-1].start()
    return made


def sent_rest_kernel(wp, wo, pp, po, n2, k2, b2, v_wp, v_wo, v_pp, v_po, v2, ok2, ob2, sems):
    top = pl.ds(0, Q)
    sources = [n2, pp.at[top], po, wp.at[top], wo.at[top]]
    loads = copies(sources, [v2, v_pp, v_po, v_wp, v_wo], sems, 0)
    for load in loads[:2]:
        load.wait()
    ob2[:Q] = dot(v_pp[...], v2[...]).astype(BF)
    loads[2].wait()
    ob2[Q:] = dot(v_po[...], v2[...]).astype(BF)
    stores = copies([ob2], [b2], sems, 5)
    loads[3].wait()
    ok2[:Q] = dot(v_wp[...], v2[...]).astype(BF)
    loads[4].wait()
    ok2[Q:] = dot(v_wo[...], v2[...]).astype(BF)
    stores += copies([ok2], [k2], sems, 6)
    for store in stores:
        store.wait()


def kept_rest_kernel(wp, pp, po, n2, g2, gb, scale, part, b01, b11, *scratch):
    v_wp, v_pp, v_po, v2, o_part, o01, o11, sems = scratch
    low = pl.ds(Q, Q)
    loads = copies([n2, po, wp.at[low], pp.at[low]], [v2, v_po, v_wp, v_pp], sems, 0)
    for load in loads[:2]:
        load.wait()
    o11[...] = ((dot(v_po[...], v2[...]) + gb[Q:]) * scale[:, WIDE:]).astype(BF)
    stores = copies([o11], [b11], sems, 4)
    loads[2].wait()
    o_part[...] = (dot(v_wp[...], v2[...]) + g2[:Q]).astype(BF)
    stores += copies([o_part], [part], sems, 5)
    loads[3].wait()
    o01[...] = ((dot(v_pp[...], v2[...]) + gb[:Q]) * scale[:, WIDE:]).astype(BF)
    stores += copies([o01], [b01], sems, 6)
    for store in stores:
        store.wait()


def scaled_kernel(left, right, got, scale, out):
    out[...] = ((dot(left[...], right[...]) + got[...]) * scale[...]).astype(BF)


def single(kernel, operands, dtype):
    shape = jax.ShapeDtypeStruct((operands[0].shape[0], operands[1].shape[1]), dtype)
    return pl.pallas_call(
        kernel,
        grid=(1,),
        out_shape=shape,
        in_specs=[whole(value) for value in operands],
        out_specs=whole(shape),
    )(*operands)


def own_kernel(left, right, got, own):
    own[...] = dot(left[...], right[...]) + got[...]


def own_product(left, right, got):
    shape = jax.ShapeDtypeStruct((Q, right.shape[1]), F32)
    return pl.pallas_call(
        own_kernel,
        grid=(1,),
        out_shape=shape,
        in_specs=[pick(left, 1), whole(right), pick(got, 1)],
        out_specs=whole(shape),
    )(left, right, got)


def vmem(*shapes):
    return [pltpu.VMEM(shape, dtype) for shape, dtype in shapes]


ANYWHERE = pl.BlockSpec(memory_space=pl.ANY)
LEFT, FAR = ((Q, R), BF), ((R, REST), BF)


def by_hand(kernel, operands, near, outs, loaded):
    shapes = [jax.ShapeDtypeStruct(*item) for item in outs]
    return pl.pallas_call(
        kernel,
        grid=(1,),
        out_shape=tuple(shapes),
        in_specs=[ANYWHERE] * len(operands) + [whole(value) for value in near],
        out_specs=(ANYWHERE,) * len(outs),
        scratch_shapes=vmem(*loaded, *outs)
        + [pltpu.SemaphoreType.DMA((len(loaded) + len(outs),))],
    )(*operands, *near)


def on_device(jacobian, obs_weight, observed, prior_state, prior_std, owner_slot):
    group = lax.axis_index("obs").astype(jnp.int32)
    block = lax.axis_index("state").astype(jnp.int32)
    half, core = group // 2, group % 2
    spread = prior_std.astype(F32)
    rows_std = lax.dynamic_slice_in_dim(spread, group * Q, Q, 0)

    next_std = over_state(prior_std, back).astype(F32)
    model = dot(jacobian, prior_state)
    n1 = columns(jacobian, 0, WIDE)
    wp = turn(jacobian, obs_weight, 1 - half, core)
    model = model + sum(over_state(model, along_z(k)) for k in range(1, 4))
    model = model + over_state(model, along_x)
    model = model + sum(over_state(model, along_y(k)) for k in range(1, 4))
    misfit = (obs_weight * (observed - model)).astype(BF)
    descent = dot(misfit, jacobian)

    def packed(slots, values):
        parts = (slots.reshape(LINES, 128), values.reshape(LINES, 128))
        return jnp.concatenate(parts + (jnp.zeros((PACKET - 2 * LINES, 128), F32),))[None]

    descent = descent + over_obs(descent, 1)
    scaled = spread * descent
    slots = owner_slot.astype(F32)
    mine = jnp.concatenate([slots, scaled])
    other = over_both(mine, 0, lambda s: s ^ 4)
    scaled = scaled + over_both(scaled, 2, lambda s: s)
    other_scaled = other[C:] + over_both(mine[C:], 2, lambda s: s ^ 4)

    scaled, other, other_scaled, wp, n1 = lax.optimization_barrier(
        (scaled, other, other_scaled, wp, n1)
    )
    packet = jnp.concatenate([packed(slots, scaled), packed(other[:C], other_scaled)])
    next1 = over_state(n1, back)
    prev_p = over_state(wp, lambda s: (s + 1) % N_STATE)
    n2 = columns(jacobian, WIDE, C - WIDE)
    wo = turn(jacobian, obs_weight, half, core)
    next2 = over_state(n2, back)
    prev_s = over_state(wo[:Q], lambda s: (s + 1) % N_STATE)
    prev_k = over_state(wo[Q:], lambda s: (s + 1) % N_STATE)
    packets = [packet]
    for _ in range(3):
        packets.append(over_state(packets[-1], ring_y))
    packet = same(jnp.concatenate(packets))
    packet = jnp.concatenate(
        [packet] + [over_state(packet, along_z(k)) for k in range(1, 4)]
    )
    gradient = place(block * C, packet)

    def exchanged(right):
        sent = product(wp, wo, right)
        got = over_obs(sent, 1)
        part, own = closing(wp, wo, right, got)
        return own, over_obs(part, 2)

    def returned(left, rights, flip, scales):
        sent, kept = split_product(left, rights)
        got = over_obs(sent, 1)
        part = ((kept + got) * scales[None, :]).astype(BF)
        return over_both(part, flip, back)

    own0, x0 = exchanged(jacobian)
    own1, x1 = exchanged(next1)
    spread = same(spread)
    rows_std = same(rows_std)
    b00 = returned(prev_p, [next1], 2, next_std[:WIDE])
    next_std = same(next_std)
    scale = next_std[None, :]
    sent1 = single(product_kernel_once, (prev_s, next1), F32)
    got1 = over_obs(sent1, 1)
    spread = same(spread)
    b10 = single(scaled_kernel, (prev_k, next1, got1, scale[:, :WIDE]), BF)
    b10 = over_both(b10, 0, back)
    operands = (wp, wo, prev_p, prev_s, next2)
    outs = [((HALF, REST), BF)] * 2
    sent2 = by_hand(sent_rest_kernel, operands, (), outs, [LEFT] * 4 + [FAR])
    got2 = [over_obs(value, 1) for value in sent2]
    operands = (wp, prev_p, prev_k, next2)
    outs = [((Q, REST), BF)] * 3
    part, b01, b11 = by_hand(
        kept_rest_kernel, operands, (*got2, scale), outs, [LEFT] * 3 + [FAR]
    )
    b11 = over_both(b11, 0, back)
    x2 = over_obs(part, 2)
    b01 = over_both(b01, 2, back)
    own2 = own_product(wo, next2, got2[0])

    parts = (own0, x0, own1, x1, b00, b10)
    band = finish(parts, rows_std, spread, next_std)
    band = finish_late(band, own2, x2, b01, b11, rows_std, next_std)
    return (jnp.transpose(band, (1, 0, 2))[None], gradient)


def solution(mesh):
    placed = (P("obs", "state"), P("obs"), P("obs"), P("state"), P("state"), P("state"))

    return jax.shard_map(
        on_device,
        mesh=mesh,
        in_specs=placed,
        out_specs=(P("state", "obs", None, None), P("state")),
        check_vma=False,
    )
```
